32 devices in a mesh: group: 4 (over z), panel: 8 (over y, x, core).
Axes of the slice: x: 2, y: 2, z: 4, core: 2. Of those that a mesh axis runs over, the one named last changes fastest.
Arguments:
- source_matrix_tiles: bfloat16 [2, 48, 4, 4096], P(None, 'group', None, 'panel'), may hold values from -6 to 6
- second_operand_encoded: bfloat16 [32, 4096, 2, 4096], P('group', None, None, 'panel'), may hold values from -0.5 to 0.5
- responding_nodes: int32 [19], replicated, may hold values from 0 to 31, as said below
Outputs:
- c_blocks: float32 [2, 48, 2, 4096], P(None, 'group', None, 'panel')
The draws below stay inside these ranges and needn't reach their ends.
Inputs may be any that keep to these rules, and one draw needn't show every extreme that they name: `responding_nodes`: 19 distinct point indices in ascending order; of the points 2 j and 2 j + 1, at least one is listed.
All inputs are finite; a program needn't handle non-finite values.
Results may differ from the reference program's by a relative error of at most 0.0029.
Values may be sent and summed in bfloat16 or wider, within the bound.
A program may use at most 192 MiB of HBM per device.

```python
import math
import jax
import jax.numpy as jnp
from jax import lax

INNER = 16384
COLS = 8192
NODE_NUMBER = 32
SURV = 19
ROWS_HALF = 48


def remaining_points(key):
    pair_count = NODE_NUMBER // 2
    lagging_pairs = NODE_NUMBER - SURV
    ranking = jax.random.permutation(jax.random.fold_in(key, 11), pair_count)
    chosen = ranking < lagging_pairs
    member = jax.random.randint(jax.random.fold_in(key, 12), (pair_count,), 0, 2)
    index = jnp.arange(NODE_NUMBER, dtype=jnp.int32)
    pair_of = index // 2
    lagging_workers = jnp.logical_and(chosen[pair_of], index % 2 == member[pair_of])
    listed_points = jnp.nonzero(jnp.logical_not(lagging_workers), size=SURV)[0].astype(jnp.int32)
    return (listed_points, lagging_workers)


def draw_responding_nodes(key, part):
    listed_points, lagging_workers = remaining_points(key)
    return listed_points


def draw_second_operand_encoded(key, part):
    quarter = INNER // 4
    half = COLS // 2
    listed_points, lagging_workers = remaining_points(key)
    blocks = jax.random.truncated_normal(jax.random.fold_in(key, 21), -4.0, 4.0, (4, 2, quarter, half), jnp.float32) / math.sqrt(INNER)
    exponent = (3.0 - jnp.arange(4, dtype=jnp.float32))[:, None] + 4.0 * jnp.arange(2, dtype=jnp.float32)[None, :]
    stale_exponent = (3.0 - jnp.arange(4, dtype=jnp.float32))[:, None] + 4.0 * (1.0 - jnp.arange(2, dtype=jnp.float32))[None, :]

    def one_point(point):
        angle = 2.0 * math.pi * point.astype(jnp.float32) / NODE_NUMBER
        stale = lagging_workers[point].astype(jnp.float32) * 0.5
        multiplier_actual = jnp.cos(angle * exponent) + stale * jnp.cos(angle * stale_exponent)
        multiplier_image = jnp.sin(angle * exponent) + stale * jnp.sin(angle * stale_exponent)
        coef = jnp.stack([multiplier_actual, multiplier_image], axis=0)
        share = jnp.einsum('klqn,ckl->qcn', blocks, coef, precision=lax.Precision.HIGHEST)
        return jnp.clip(share, -0.5, 0.5).astype(jnp.bfloat16)
    return lax.map(one_point, jnp.arange(NODE_NUMBER, dtype=jnp.int32))


def block_scale(key, extent, cuts, least, high):
    gain = 1.0
    for dim, blocks in cuts:
        heights = jax.random.uniform(jax.random.fold_in(jax.random.fold_in(key, 6), dim), (blocks,), jnp.float32, least / len(cuts), high / len(cuts))
        gain = gain * jnp.repeat(jnp.exp(heights), extent[dim] // blocks).reshape((-1,) + (1,) * (len(extent) - 1 - dim))
    return gain


def centred(rng, shape, scale, most, pieces=(), kind=jnp.bfloat16):
    factor_of = block_scale(rng, shape, pieces, -0.22, 0.18) if pieces else 1.0
    values = jax.random.normal(rng, shape, jnp.float32) * scale * factor_of
    return jnp.minimum(jnp.maximum(values, -most), most).astype(kind)


def setup_inputs(seed: int = 0) -> dict:
    key_of = jax.random.split(jax.random.key(seed), 4)
    source_matrix_tiles = centred(key_of[0], (2, ROWS_HALF, 4, INNER // 4), 1.0, 6.0, ((1, 4), (3, 8)))
    second_operand_encoded = draw_second_operand_encoded(jax.random.fold_in(key_of[3], 71), 0)
    responding_nodes = draw_responding_nodes(jax.random.fold_in(key_of[3], 71), 0)
    return {"source_matrix_tiles": source_matrix_tiles, "second_operand_encoded": second_operand_encoded, "responding_nodes": responding_nodes}


TWO_PI_RADIANS = 2.0 * math.pi


def point_trig(node_phases):
    exponent = jnp.arange(4, dtype=jnp.float32)[None, :] + 8.0 * jnp.arange(2, dtype=jnp.float32)[:, None]
    phase = node_phases[:, None, None] * exponent[None]
    return jnp.stack([jnp.cos(phase), jnp.sin(phase)], axis=1)


def recovery_coefficients(responding_nodes):
    responder_number = responding_nodes.shape[0]
    grid_index = jnp.arange(NODE_NUMBER, dtype=jnp.int32)
    grid_angle = TWO_PI_RADIANS * grid_index.astype(jnp.float32) / NODE_NUMBER
    node_angle = TWO_PI_RADIANS * responding_nodes.astype(jnp.float32) / NODE_NUMBER
    diff_real = jnp.cos(grid_angle)[None, :] - jnp.cos(node_angle)[:, None]
    diff_imag = jnp.sin(grid_angle)[None, :] - jnp.sin(node_angle)[:, None]
    ranks = jnp.arange(responder_number, dtype=jnp.int32)
    itself = (ranks[:, None] == ranks[None, :])[:, :, None]
    factor_real = jnp.where(itself, jnp.float32(1.0), diff_real[None])
    factor_imag = jnp.where(itself, jnp.float32(0.0), diff_imag[None])
    padded_width = 1 << (responder_number - 1).bit_length()
    extra = padded_width - responder_number
    factor_real = jnp.concatenate(
        [factor_real, jnp.ones((responder_number, extra, NODE_NUMBER), jnp.float32)], axis=1)
    factor_imag = jnp.concatenate(
        [factor_imag, jnp.zeros((responder_number, extra, NODE_NUMBER), jnp.float32)], axis=1)
    while factor_real.shape[1] > 1:
        middle = factor_real.shape[1] // 2
        left_real, right_real = factor_real[:, :middle], factor_real[:, middle:]
        left_imag, right_imag = factor_imag[:, :middle], factor_imag[:, middle:]
        factor_real = left_real * right_real - left_imag * right_imag
        factor_imag = left_real * right_imag + left_imag * right_real
    sample_real = factor_real[:, 0]
    sample_imag = factor_imag[:, 0]
    wanted = 3.0 + 4.0 * jnp.arange(4, dtype=jnp.float32)
    table_angle = -grid_angle[:, None] * wanted[None, :]
    table_cos = jnp.cos(table_angle)
    table_sin = jnp.sin(table_angle)
    highest = lax.Precision.HIGHEST
    numer_real = (jnp.dot(sample_real, table_cos, precision=highest) - jnp.dot(sample_imag, table_sin, precision=highest)) / NODE_NUMBER
    numer_imag = (jnp.dot(sample_real, table_sin, precision=highest) + jnp.dot(sample_imag, table_cos, precision=highest)) / NODE_NUMBER
    onehot = (responding_nodes[:, None] == grid_index[None, :]).astype(jnp.float32)
    denom_real = jnp.sum(onehot * sample_real, axis=1)
    denom_imag = jnp.sum(onehot * sample_imag, axis=1)
    magnitude = denom_real * denom_real + denom_imag * denom_imag
    coefficient_actual = (numer_real * denom_real[:, None] + numer_imag * denom_imag[:, None]) / magnitude[:, None]
    coefficient_image = (numer_imag * denom_real[:, None] - numer_real * denom_imag[:, None]) / magnitude[:, None]
    return coefficient_actual, coefficient_image


def reference(source_matrix_tiles, second_operand_encoded, responding_nodes):
    coefficient_actual, coefficient_image = recovery_coefficients(responding_nodes)
    rows_half = source_matrix_tiles.shape[1]
    quarter = source_matrix_tiles.shape[3]
    cols_half = second_operand_encoded.shape[3]
    a_wide = source_matrix_tiles.astype(jnp.float32)

    def gather_matrix_sum(running, inputs):
        point, real_row, imag_row = inputs
        node_phases = TWO_PI_RADIANS * point.astype(jnp.float32)[None] / NODE_NUMBER
        trig = point_trig(node_phases)[0]
        coded = jnp.einsum("irkn,cik->crn", a_wide, trig, precision=lax.Precision.HIGHEST).astype(jnp.bfloat16)
        share = lax.dynamic_index_in_dim(second_operand_encoded, point, 0, keepdims=False)
        product = jnp.dot(coded.reshape(2 * rows_half, quarter), share.reshape(quarter, 2 * cols_half),
                          preferred_element_type=jnp.float32)
        real_part = product[:rows_half, :cols_half] - product[rows_half:, cols_half:]
        imag_part = product[:rows_half, cols_half:] + product[rows_half:, :cols_half]
        term = jnp.einsum("il,rn->irln", real_row.reshape(2, 2), real_part, precision=lax.Precision.HIGHEST)
        term = term - jnp.einsum("il,rn->irln", imag_row.reshape(2, 2), imag_part, precision=lax.Precision.HIGHEST)
        return running + term, None

    starting_carry = jnp.zeros((2, rows_half, 2, cols_half), jnp.float32)
    output_matrix, ignored_element = lax.scan(gather_matrix_sum, starting_carry, (responding_nodes.astype(jnp.int32), coefficient_actual, coefficient_image))
    return output_matrix
```

```python
import functools
import math

import jax
import jax.numpy as jnp
from jax import lax
from jax.experimental import pallas as pl
from jax.experimental.pallas import tpu as pltpu
from jax.sharding import PartitionSpec as P

NODE_NUMBER = 32
TWO_PI_RADIANS = 2.0 * math.pi
LANES = 128
DEPTH = 12


def point_trig(node_phases):
    exponent = (
        jnp.arange(4, dtype=jnp.float32)[None, :] + 8.0 * jnp.arange(2, dtype=jnp.float32)[:, None]
    )
    phase = node_phases[:, None, None] * exponent[None]
    return jnp.stack([jnp.cos(phase), jnp.sin(phase)], axis=1)


def recovery_coefficients(responding_nodes):
    responder_number = responding_nodes.shape[0]
    grid_index = jnp.arange(NODE_NUMBER, dtype=jnp.int32)
    grid_angle = TWO_PI_RADIANS * grid_index.astype(jnp.float32) / NODE_NUMBER
    node_angle = TWO_PI_RADIANS * responding_nodes.astype(jnp.float32) / NODE_NUMBER
    diff_real = jnp.cos(grid_angle)[None, :] - jnp.cos(node_angle)[:, None]
    diff_imag = jnp.sin(grid_angle)[None, :] - jnp.sin(node_angle)[:, None]
    ranks = jnp.arange(responder_number, dtype=jnp.int32)
    itself = (ranks[:, None] == ranks[None, :])[:, :, None]
    factor_real = jnp.where(itself, jnp.float32(1.0), diff_real[None])
    factor_imag = jnp.where(itself, jnp.float32(0.0), diff_imag[None])
    padded_width = 1 << (responder_number - 1).bit_length()
    extra = padded_width - responder_number
    factor_real = jnp.concatenate(
        [factor_real, jnp.ones((responder_number, extra, NODE_NUMBER), jnp.float32)], axis=1
    )
    factor_imag = jnp.concatenate(
        [factor_imag, jnp.zeros((responder_number, extra, NODE_NUMBER), jnp.float32)], axis=1
    )
    while factor_real.shape[1] > 1:
        middle = factor_real.shape[1] // 2
        left_real, right_real = (factor_real[:, :middle], factor_real[:, middle:])
        left_imag, right_imag = (factor_imag[:, :middle], factor_imag[:, middle:])
        factor_real = left_real * right_real - left_imag * right_imag
        factor_imag = left_real * right_imag + left_imag * right_real
    sample_real = factor_real[:, 0]
    sample_imag = factor_imag[:, 0]
    wanted = 3.0 + 4.0 * jnp.arange(4, dtype=jnp.float32)
    table_angle = -grid_angle[:, None] * wanted[None, :]
    table_cos = jnp.cos(table_angle)
    table_sin = jnp.sin(table_angle)
    highest = lax.Precision.HIGHEST
    numer_real = (
        jnp.dot(sample_real, table_cos, precision=highest)
        - jnp.dot(sample_imag, table_sin, precision=highest)
    ) / NODE_NUMBER
    numer_imag = (
        jnp.dot(sample_real, table_sin, precision=highest)
        + jnp.dot(sample_imag, table_cos, precision=highest)
    ) / NODE_NUMBER
    onehot = (responding_nodes[:, None] == grid_index[None, :]).astype(jnp.float32)
    denom_real = jnp.sum(onehot * sample_real, axis=1)
    denom_imag = jnp.sum(onehot * sample_imag, axis=1)
    magnitude = denom_real * denom_real + denom_imag * denom_imag
    coefficient_actual = (
        numer_real * denom_real[:, None] + numer_imag * denom_imag[:, None]
    ) / magnitude[:, None]
    coefficient_image = (
        numer_imag * denom_real[:, None] - numer_real * denom_imag[:, None]
    ) / magnitude[:, None]
    return (coefficient_actual, coefficient_image)


def product_kernel(
    count_ref, order_ref, trig_ref, weight_ref, a_ref, spread_ref, b_ref, out_ref, buf, acc, sems
):
    rows, inner = a_ref.shape[1], a_ref.shape[2]
    tiles = b_ref.shape[2]
    depth, _, kb = buf.shape[0], buf.shape[1], buf.shape[2]
    blocks = inner // kb
    total = count_ref[0] * blocks

    def copies(step):
        point = order_ref[step // blocks]
        start = pl.multiple_of((step % blocks) * kb, kb)
        slot = step % depth
        return [
            pltpu.make_async_copy(
                b_ref.at[point, pl.ds(start, kb), t], buf.at[slot, t], sems.at[slot, t]
            )
            for t in range(tiles)
        ]

    def fetch(step):
        @pl.when(step < total)
        def _():
            for copy in copies(step):
                copy.start()

    for step in range(depth - 1):
        fetch(step)
    out_ref[...] = jnp.zeros_like(out_ref)

    def body(step, carry):
        fetch(step + depth - 1)
        point = order_ref[step // blocks]
        block = step % blocks
        start = pl.multiple_of(block * kb, kb)
        real = jnp.zeros((rows, kb), jnp.float32)
        imag = jnp.zeros((rows, kb), jnp.float32)
        for e in range(a_ref.shape[0]):
            piece = a_ref[e, :, pl.ds(start, kb)].astype(jnp.float32)
            real = real + piece * trig_ref[point, e]
            imag = imag + piece * trig_ref[point, a_ref.shape[0] + e]
        real = real.astype(jnp.bfloat16)
        imag = imag.astype(jnp.bfloat16)
        parts = []
        for t in range(kb // LANES):
            r = real[:, t * LANES : (t + 1) * LANES]
            i = imag[:, t * LANES : (t + 1) * LANES]
            parts.append(jnp.concatenate([r, -i], axis=1))
            parts.append(jnp.concatenate([i, r], axis=1))
        mixed = jnp.dot(
            jnp.concatenate(parts, axis=0), spread_ref[...], preferred_element_type=jnp.float32
        ).astype(jnp.bfloat16)
        left = jnp.concatenate(
            [mixed[2 * rows * t : 2 * rows * (t + 1)] for t in range(kb // LANES)], axis=1
        )
        for copy in copies(step):
            copy.wait()
        slot = step % depth
        right = jnp.concatenate(
            [buf[slot, t].reshape(2 * kb, LANES) for t in range(tiles)], axis=1
        )
        product = jnp.dot(left, right, preferred_element_type=jnp.float32)
        value = jnp.where(block == 0, product, acc[...] + product)
        acc[...] = value

        @pl.when(block == blocks - 1)
        def _():
            for e in range(4):
                out_ref[e] += (
                    weight_ref[point, e] * value[:rows] - weight_ref[point, 4 + e] * value[rows:]
                )

        return carry

    lax.fori_loop(0, total, body, 0)


def weighted_product(count, order, trig, weight, whole, shares):
    here, inner, tiles = shares.shape[0], shares.shape[1], shares.shape[2]
    rows = whole.shape[1]
    kb = min(inner, 512)
    index = jnp.arange(2 * LANES)
    target = jnp.where(index < LANES, 2 * index, 2 * (index - LANES) + 1)
    spread = (target[:, None] == index[None, :]).astype(jnp.bfloat16)
    smem = pl.BlockSpec(memory_space=pltpu.SMEM)
    vmem = pl.BlockSpec(memory_space=pltpu.VMEM)
    return pl.pallas_call(
        product_kernel,
        out_shape=jax.ShapeDtypeStruct((4, rows, tiles * LANES), jnp.float32),
        in_specs=[smem, smem, smem, smem, vmem, vmem, pl.BlockSpec(memory_space=pl.ANY)],
        out_specs=vmem,
        scratch_shapes=[
            pltpu.VMEM((DEPTH, tiles, kb, 2, LANES), jnp.bfloat16),
            pltpu.VMEM((2 * rows, tiles * LANES), jnp.float32),
            pltpu.SemaphoreType.DMA((DEPTH, tiles)),
        ],
        compiler_params=pltpu.CompilerParams(vmem_limit_bytes=50 << 20),
    )(count, order, trig, weight, whole, spread, shares)


def shards(source_matrix_tiles, second_operand_encoded, responding_nodes):
    coefficient_actual, coefficient_image = recovery_coefficients(responding_nodes)
    here, inner, _, cols = second_operand_encoded.shape
    first_point = lax.axis_index("group") * here
    points = first_point + jnp.arange(here, dtype=jnp.int32)
    selector = (responding_nodes[:, None] == points[None, :]).astype(jnp.float32)
    highest = lax.Precision.HIGHEST
    weight = jnp.concatenate(
        [
            jnp.dot(selector.T, coefficient_actual, precision=highest),
            jnp.dot(selector.T, coefficient_image, precision=highest),
        ],
        axis=1,
    )
    listed = jnp.any(responding_nodes[:, None] == points[None, :], axis=0)
    rank = jnp.cumsum(listed.astype(jnp.int32)) - 1
    local = jnp.arange(here, dtype=jnp.int32)
    order = jnp.sum(
        jnp.where(listed[None, :] & (rank[None, :] == local[:, None]), local[None, :], 0), axis=1
    )
    count = jnp.sum(listed.astype(jnp.int32))[None]
    trig = point_trig(TWO_PI_RADIANS * points.astype(jnp.float32) / NODE_NUMBER)
    trig = trig.reshape(here, 16)
    whole = lax.all_gather(source_matrix_tiles, "group", axis=1, tiled=True)
    whole = lax.all_gather(whole, "panel", axis=3, tiled=True)
    rows = whole.shape[1]
    whole = whole.transpose(0, 2, 1, 3).reshape(8, rows, inner)
    shares = second_operand_encoded.reshape(here, inner, 2, cols // LANES, LANES)
    shares = shares.transpose(0, 1, 3, 2, 4)
    partial_sum = weighted_product(count, order, trig, weight, whole, shares)
    partial_sum = partial_sum.reshape(2, 2, rows, cols).transpose(0, 2, 1, 3)
    return lax.psum_scatter(partial_sum, "group", scatter_dimension=1, tiled=True)


def solution(mesh):
    placed = (P(None, "group", None, "panel"), P("group", None, None, "panel"), P())
    return jax.shard_map(
        shards,
        mesh=mesh,
        in_specs=placed,
        out_specs=P(None, "group", None, "panel"),
        check_vma=False,
    )
```

```python
import functools
import math

import jax
import jax.numpy as jnp
from jax import lax
from jax.experimental import pallas as pl
from jax.experimental.pallas import tpu as pltpu
from jax.sharding import PartitionSpec as P

NODE_NUMBER = 32
TWO_PI_RADIANS = 2.0 * math.pi
LANES = 128
DEPTH = 12
MESH = pl.DeviceIdType.MESH


def point_trig(node_phases):
    exponent = (
        jnp.arange(4, dtype=jnp.float32)[None, :] + 8.0 * jnp.arange(2, dtype=jnp.float32)[:, None]
    )
    phase = node_phases[:, None, None] * exponent[None]
    return jnp.stack([jnp.cos(phase), jnp.sin(phase)], axis=1)


def recovery_coefficients(responding_nodes):
    responder_number = responding_nodes.shape[0]
    grid_index = jnp.arange(NODE_NUMBER, dtype=jnp.int32)
    grid_angle = TWO_PI_RADIANS * grid_index.astype(jnp.float32) / NODE_NUMBER
    node_angle = TWO_PI_RADIANS * responding_nodes.astype(jnp.float32) / NODE_NUMBER
    diff_real = jnp.cos(grid_angle)[None, :] - jnp.cos(node_angle)[:, None]
    diff_imag = jnp.sin(grid_angle)[None, :] - jnp.sin(node_angle)[:, None]
    ranks = jnp.arange(responder_number, dtype=jnp.int32)
    itself = (ranks[:, None] == ranks[None, :])[:, :, None]
    factor_real = jnp.where(itself, jnp.float32(1.0), diff_real[None])
    factor_imag = jnp.where(itself, jnp.float32(0.0), diff_imag[None])
    padded_width = 1 << (responder_number - 1).bit_length()
    extra = padded_width - responder_number
    factor_real = jnp.concatenate(
        [factor_real, jnp.ones((responder_number, extra, NODE_NUMBER), jnp.float32)], axis=1
    )
    factor_imag = jnp.concatenate(
        [factor_imag, jnp.zeros((responder_number, extra, NODE_NUMBER), jnp.float32)], axis=1
    )
    while factor_real.shape[1] > 1:
        middle = factor_real.shape[1] // 2
        left_real, right_real = (factor_real[:, :middle], factor_real[:, middle:])
        left_imag, right_imag = (factor_imag[:, :middle], factor_imag[:, middle:])
        factor_real = left_real * right_real - left_imag * right_imag
        factor_imag = left_real * right_imag + left_imag * right_real
    sample_real = factor_real[:, 0]
    sample_imag = factor_imag[:, 0]
    wanted = 3.0 + 4.0 * jnp.arange(4, dtype=jnp.float32)
    table_angle = -grid_angle[:, None] * wanted[None, :]
    table_cos = jnp.cos(table_angle)
    table_sin = jnp.sin(table_angle)
    highest = lax.Precision.HIGHEST
    numer_real = (
        jnp.dot(sample_real, table_cos, precision=highest)
        - jnp.dot(sample_imag, table_sin, precision=highest)
    ) / NODE_NUMBER
    numer_imag = (
        jnp.dot(sample_real, table_sin, precision=highest)
        + jnp.dot(sample_imag, table_cos, precision=highest)
    ) / NODE_NUMBER
    onehot = (responding_nodes[:, None] == grid_index[None, :]).astype(jnp.float32)
    denom_real = jnp.sum(onehot * sample_real, axis=1)
    denom_imag = jnp.sum(onehot * sample_imag, axis=1)
    magnitude = denom_real * denom_real + denom_imag * denom_imag
    coefficient_actual = (
        numer_real * denom_real[:, None] + numer_imag * denom_imag[:, None]
    ) / magnitude[:, None]
    coefficient_image = (
        numer_imag * denom_real[:, None] - numer_real * denom_imag[:, None]
    ) / magnitude[:, None]
    return (coefficient_actual, coefficient_image)


def relatives(panel):
    core, east, north = panel % 2, (panel // 2) % 2, panel // 4
    return panel + 1 - 2 * core, panel + 2 - 4 * east, panel + 4 - 8 * north


def gather_kernel(own_ref, out_ref, send_far, send_x, send_y, send_on, send_core, recv, local):
    group, panel = lax.axis_index("group"), lax.axis_index("panel")
    groups = lax.axis_size("group")
    part = own_ref.shape[1]
    core = panel % 2
    mate, east, north = relatives(panel)
    across = relatives(east)[2]
    forward_from = north + core * (east - north)
    forward_to = east + core * (north - east)

    def slot(p, g):
        return out_ref.at[p, :, pl.ds(g * part, part)]

    def copy(p, g, send_sem, target, source=None):
        return pltpu.make_async_remote_copy(
            src_ref=slot(p, g) if source is None else source,
            dst_ref=slot(p, g),
            send_sem=send_sem,
            recv_sem=recv.at[p, g],
            device_id=target,
            device_id_type=MESH,
        )

    def arrive(p, g):
        copy(p, g, send_far.at[0], (group, mate)).wait_recv()

    barrier = pltpu.get_barrier_semaphore()
    peers = [(group, mate), (group, east), (group, north)]
    peers += [(lax.rem(group + d, groups), panel) for d in range(1, groups)]
    for peer in peers:
        pl.semaphore_signal(barrier, inc=1, device_id=peer, device_id_type=MESH)
    keep = pltpu.make_async_copy(own_ref, slot(panel, group), local)
    keep.start()
    pl.semaphore_wait(barrier, len(peers))
    sent = []

    def send(*args):
        sent.append(copy(*args))
        sent[-1].start()

    for d in range(1, groups):
        send(panel, group, send_far.at[d - 1], (lax.rem(group + d, groups), panel), own_ref)
    order = [lax.rem(group + d, groups) for d in range(groups)]
    for d, g in enumerate(order):
        source = own_ref if d == 0 else None
        if d:
            arrive(panel, g)
        send(panel, g, send_x.at[d], (group, east), source)
        send(panel, g, send_y.at[d], (group, north), source)
        send(panel, g, send_core.at[0, d], (group, mate), source)
        arrive(forward_from, g)
        send(forward_from, g, send_on.at[d], (group, forward_to))
        send(forward_from, g, send_core.at[1, d], (group, mate))
        arrive(forward_to, g)
        send(forward_to, g, send_core.at[2, d], (group, mate))
    for d, g in enumerate(order):
        arrive(across, g)
        send(across, g, send_core.at[3, d], (group, mate))
    for p in (mate,) + relatives(mate)[1:] + (relatives(across)[0],):
        for g in order:
            arrive(p, g)
    for item in sent:
        item.wait_send()
    keep.wait()


def gather(own, groups, panels):
    part = own.shape[1]
    any_space = pl.BlockSpec(memory_space=pl.ANY)
    dma = pltpu.SemaphoreType.DMA
    return pl.pallas_call(
        gather_kernel,
        out_shape=jax.ShapeDtypeStruct(
            (panels, own.shape[0], groups * part) + own.shape[2:], own.dtype
        ),
        in_specs=[any_space],
        out_specs=any_space,
        scratch_shapes=[
            dma((groups - 1,)), dma((groups,)), dma((groups,)), dma((groups,)),
            dma((4, groups)), dma((panels, groups)), dma,
        ],
        compiler_params=pltpu.CompilerParams(collective_id=0, has_side_effects=True),
    )(own)


def exchange_kernel(part_ref, out_ref, send, recv, local):
    group, panel = lax.axis_index("group"), lax.axis_index("panel")
    groups = lax.axis_size("group")
    part = out_ref.shape[2]
    barrier = pltpu.get_barrier_semaphore()
    peers = [lax.rem(group + d, groups) for d in range(1, groups)]
    for peer in peers:
        pl.semaphore_signal(barrier, inc=1, device_id=(peer, panel), device_id_type=MESH)
    keep = pltpu.make_async_copy(part_ref.at[:, pl.ds(group * part, part)], out_ref.at[0], local)
    keep.start()
    pl.semaphore_wait(barrier, len(peers))
    copies = [
        pltpu.make_async_remote_copy(
            src_ref=part_ref.at[:, pl.ds(peer * part, part)],
            dst_ref=out_ref.at[d + 1],
            send_sem=send.at[d],
            recv_sem=recv.at[d],
            device_id=(peer, panel),
            device_id_type=MESH,
        )
        for d, peer in enumerate(peers)
    ]
    for copy in copies:
        copy.start()
    for copy in copies:
        copy.wait()
    keep.wait()


def exchange(parts, groups):
    any_space = pl.BlockSpec(memory_space=pl.ANY)
    dma = pltpu.SemaphoreType.DMA
    slots, rows = parts.shape[0], parts.shape[1]
    return pl.pallas_call(
        exchange_kernel,
        out_shape=jax.ShapeDtypeStruct(
            (groups, slots, rows // groups) + parts.shape[2:], parts.dtype
        ),
        in_specs=[any_space],
        out_specs=any_space,
        scratch_shapes=[dma((groups - 1,)), dma((groups - 1,)), dma],
        compiler_params=pltpu.CompilerParams(collective_id=1, has_side_effects=True),
    )(parts)


def product_kernel(
    count_ref, order_ref, trig_ref, weight_ref, whole_ref, spread_ref, share_ref, out_ref,
    a_ref, buf, acc, total_ref, sems, a_sems, out_sem,
):
    blocks, pieces, rows, kb = a_ref.shape
    depth, cols = buf.shape[0], buf.shape[2]
    b_ref = share_ref.reshape(share_ref.shape[0], 2 * blocks * kb, cols)
    total = count_ref[0] * blocks

    def copy(step):
        start = pl.multiple_of((step % blocks) * 2 * kb, 2 * kb)
        slot = step % depth
        return pltpu.make_async_copy(
            b_ref.at[order_ref[step // blocks], pl.ds(start, 2 * kb)], buf.at[slot], sems.at[slot]
        )

    def take(block):
        return pltpu.make_async_copy(
            whole_ref.at[block].reshape(pieces, rows, kb), a_ref.at[block], a_sems.at[block]
        )

    def fetch(step):
        @pl.when(step < total)
        def _():
            copy(step).start()

    fetch(0)
    for block in range(blocks):
        take(block).start()
    for step in range(1, depth - 1):
        fetch(step)
    total_ref[...] = jnp.zeros_like(total_ref)
    for block in range(blocks):
        take(block).wait()

    def body(step, carry):
        fetch(step + depth - 1)
        copy(step).wait()
        point = order_ref[step // blocks]
        block = step % blocks
        slot = step % depth
        real = jnp.zeros((rows, kb), jnp.float32)
        imag = jnp.zeros((rows, kb), jnp.float32)
        for e in range(pieces):
            piece = a_ref[block, e].astype(jnp.float32)
            real = real + piece * trig_ref[point, e]
            imag = imag + piece * trig_ref[point, pieces + e]
        real = real.astype(jnp.bfloat16)
        imag = imag.astype(jnp.bfloat16)
        parts = []
        for t in range(kb // LANES):
            r = real[:, t * LANES : (t + 1) * LANES]
            i = imag[:, t * LANES : (t + 1) * LANES]
            parts.append(jnp.concatenate([r, -i], axis=1))
            parts.append(jnp.concatenate([i, r], axis=1))
        mixed = jnp.dot(
            jnp.concatenate(parts, axis=0), spread_ref[...], preferred_element_type=jnp.float32
        ).astype(jnp.bfloat16)
        left = jnp.concatenate(
            [mixed[2 * rows * t : 2 * rows * (t + 1)] for t in range(kb // LANES)], axis=1
        )
        product = jnp.dot(left, buf[slot], preferred_element_type=jnp.float32)
        acc[...] = jnp.where(block == 0, product, acc[...] + product)

        @pl.when(block == blocks - 1)
        def _():
            for e in range(4):
                total_ref[e] += (
                    weight_ref[point, e] * acc[:rows] - weight_ref[point, 4 + e] * acc[rows:]
                )

        return carry

    lax.fori_loop(0, total, body, 0)
    done = pltpu.make_async_copy(total_ref, out_ref.reshape(*total_ref.shape), out_sem)
    done.start()
    done.wait()


def weighted_product(count, order, trig, weight, whole, shares):
    cols = shares.shape[3]
    blocks, pieces, row_tiles, tile, kb = whole.shape
    rows = row_tiles * tile
    index = jnp.arange(2 * LANES)
    target = jnp.where(index < LANES, 2 * index, 2 * (index - LANES) + 1)
    spread = (target[:, None] == index[None, :]).astype(jnp.bfloat16)
    smem = pl.BlockSpec(memory_space=pltpu.SMEM)
    any_space = pl.BlockSpec(memory_space=pl.ANY)
    return pl.pallas_call(
        product_kernel,
        out_shape=jax.ShapeDtypeStruct((4, row_tiles, tile, cols), jnp.float32),
        in_specs=[
            smem, smem, smem, smem, any_space, pl.BlockSpec(memory_space=pltpu.VMEM), any_space,
        ],
        out_specs=any_space,
        scratch_shapes=[
            pltpu.VMEM((blocks, pieces, rows, kb), jnp.bfloat16),
            pltpu.VMEM((DEPTH, 2 * kb, cols), jnp.bfloat16),
            pltpu.VMEM((2 * rows, cols), jnp.float32),
            pltpu.VMEM((4, rows, cols), jnp.float32),
            pltpu.SemaphoreType.DMA((DEPTH,)),
            pltpu.SemaphoreType.DMA((blocks,)),
            pltpu.SemaphoreType.DMA,
        ],
        compiler_params=pltpu.CompilerParams(vmem_limit_bytes=50 << 20),
    )(count, order, trig, weight, whole, spread, shares)


def shards(own_kernels, groups, panels, source_matrix_tiles, shares, responding_nodes):
    coefficient_actual, coefficient_image = recovery_coefficients(responding_nodes)
    here, cols = shares.shape[0], shares.shape[3]
    points = lax.axis_index("group") * here + jnp.arange(here, dtype=jnp.int32)
    selector = (responding_nodes[:, None] == points[None, :]).astype(jnp.float32)
    highest = lax.Precision.HIGHEST
    weight = jnp.concatenate(
        [
            jnp.dot(selector.T, coefficient_actual, precision=highest),
            jnp.dot(selector.T, coefficient_image, precision=highest),
        ],
        axis=1,
    )
    listed = jnp.any(responding_nodes[:, None] == points[None, :], axis=0)
    local = jnp.arange(here, dtype=jnp.int32)
    rank = jnp.sum((local[None, :] < local[:, None]) & listed[None, :], axis=1)
    order = jnp.sum(
        jnp.where(listed[None, :] & (rank[None, :] == local[:, None]), local[None, :], 0), axis=1
    )
    count = jnp.sum(listed.astype(jnp.int32))[None]
    trig = point_trig(TWO_PI_RADIANS * points.astype(jnp.float32) / NODE_NUMBER)
    trig = trig.reshape(here, 16)
    _, rows, _, kb = source_matrix_tiles.shape
    tile = math.gcd(rows, 4)
    own = source_matrix_tiles.transpose(0, 2, 1, 3).reshape(8, rows // tile, tile, kb)
    if own_kernels:
        whole = gather(own, groups, panels)
    else:
        whole = lax.all_gather(own, "group", axis=1, tiled=True)
        whole = lax.all_gather(whole, "panel", axis=0)
    parts = weighted_product(count, order, trig, weight, whole, shares)
    if own_kernels:
        result = jnp.sum(exchange(parts, groups), axis=0)
    else:
        result = lax.psum_scatter(parts, "group", scatter_dimension=1, tiled=True)
    return result.reshape(2, 2, rows, cols).transpose(0, 2, 1, 3)


def solution(mesh):
    placed = (P(None, "group", None, "panel"), P("group", None, None, "panel"), P())
    groups, panels = mesh.shape["group"], mesh.shape["panel"]
    return jax.shard_map(
        functools.partial(shards, panels == 8, groups, panels),
        mesh=mesh,
        in_specs=placed,
        out_specs=P(None, "group", None, "panel"),
        check_vma=False,
    )
```

```python
import functools
import math

import jax
import jax.numpy as jnp
import numpy as np
from jax import lax
from jax.experimental import pallas as pl
from jax.experimental.pallas import tpu as pltpu
from jax.sharding import PartitionSpec as P

NODE_NUMBER = 32
TWO_PI_RADIANS = 2.0 * math.pi
LANES = 128
DEPTH = 12
MESH = pl.DeviceIdType.MESH


def tables():
    grid = np.arange(NODE_NUMBER)
    angle = TWO_PI_RADIANS * grid / NODE_NUMBER
    ring = np.zeros((2, LANES), np.float32)
    ring[0, :NODE_NUMBER], ring[1, :NODE_NUMBER] = np.cos(angle), np.sin(angle)
    wanted = 3 + 4 * np.arange(4)
    turn = -TWO_PI_RADIANS * ((grid[None, :] * wanted[:, None]) % NODE_NUMBER) / NODE_NUMBER
    wave = np.zeros((8, LANES), np.float32)
    wave[:4, :NODE_NUMBER], wave[4:, :NODE_NUMBER] = np.cos(turn), np.sin(turn)
    return ring, wave / NODE_NUMBER


def weight_kernel(nodes_ref, ring_ref, wave_ref, out_ref):
    here = out_ref.shape[0]
    listed = nodes_ref.shape[0]
    first = lax.axis_index("group") * here
    lane = lax.broadcasted_iota(jnp.int32, (here, LANES), 1)
    point = lax.broadcasted_iota(jnp.int32, (here, LANES), 0) + first
    ring_real = jnp.broadcast_to(ring_ref[0:1, :], (here, LANES))
    ring_imag = jnp.broadcast_to(ring_ref[1:2, :], (here, LANES))

    def at(table, index):
        return jnp.sum(jnp.where(lane == index, table, 0.0), axis=1, keepdims=True)

    factors = []
    found = jnp.zeros((here, LANES), jnp.float32)
    for t in range(listed):
        node = nodes_ref[t]
        same = point == node
        found = jnp.where(same, 1.0, found)
        real = ring_real - at(ring_real, node)
        imag = ring_imag - at(ring_imag, node)
        factors.append((jnp.where(same, 1.0, real), jnp.where(same, 0.0, imag)))
    while len(factors) > 1:
        middle = (len(factors) + 1) // 2
        joined = [
            (p * r - q * i, p * i + q * r)
            for (p, q), (r, i) in zip(factors[: len(factors) - middle], factors[middle:])
        ]
        factors = joined + factors[len(factors) - middle : middle]
    real, imag = factors[0]
    under_real = at(real, point)
    under_imag = at(imag, point)
    size = under_real * under_real + under_imag * under_imag
    present = found[:, :1] > 0.5
    size = jnp.where(present, size, 1.0)
    outcome = jnp.zeros((here, LANES), jnp.float32)
    for e in range(4):
        cosine, sine = wave_ref[e : e + 1, :], wave_ref[4 + e : 5 + e, :]
        over_real = jnp.sum(real * cosine - imag * sine, axis=1, keepdims=True)
        over_imag = jnp.sum(real * sine + imag * cosine, axis=1, keepdims=True)
        weight_real = (over_real * under_real + over_imag * under_imag) / size
        weight_imag = (over_imag * under_real - over_real * under_imag) / size
        outcome = jnp.where(lane == e, jnp.where(present, weight_real, 0.0), outcome)
        outcome = jnp.where(lane == 4 + e, jnp.where(present, weight_imag, 0.0), outcome)
    out_ref[...] = outcome


def local_weights(nodes, here):
    ring, wave = tables()
    vmem = pl.BlockSpec(memory_space=pltpu.VMEM)
    return pl.pallas_call(
        weight_kernel,
        out_shape=jax.ShapeDtypeStruct((here, LANES), jnp.float32),
        in_specs=[pl.BlockSpec(memory_space=pltpu.SMEM), vmem, vmem],
        out_specs=vmem,
    )(nodes, jnp.asarray(ring), jnp.asarray(wave))


def relatives(panel):
    core, east, north = panel % 2, (panel // 2) % 2, panel // 4
    return panel + 1 - 2 * core, panel + 2 - 4 * east, panel + 4 - 8 * north


def gather_kernel(own_ref, out_ref, send_z, send_x, send_y, send_on, send_core, recv, local):
    group, panel = lax.axis_index("group"), lax.axis_index("panel")
    groups = lax.axis_size("group")
    part = own_ref.shape[1]
    core = panel % 2
    mate, east, north = relatives(panel)
    across = relatives(east)[2]
    forward_from = north + core * (east - north)
    forward_to = east + core * (north - east)

    def run(me):
        def slot(p, g):
            return out_ref.at[p, :, pl.ds(g * part, part)]

        def copy(p, g, send_sem, target):
            return pltpu.make_async_remote_copy(
                src_ref=own_ref if p is panel and g == me else slot(p, g),
                dst_ref=slot(p, g),
                send_sem=send_sem,
                recv_sem=recv.at[p, g],
                device_id=target,
                device_id_type=MESH,
            )

        def arrive(p, g):
            copy(p, g, send_z.at[0, 0], (me, mate)).wait_recv()

        sent = []

        def send(*args):
            sent.append(copy(*args))
            sent[-1].start()

        barrier = pltpu.get_barrier_semaphore()
        chain = [g for g in (me - 1, me + 1) if 0 <= g < groups]
        peers = [(me, mate), (me, east), (me, north)] + [(g, panel) for g in chain]
        for peer in peers:
            pl.semaphore_signal(barrier, inc=1, device_id=peer, device_id_type=MESH)
        keep = pltpu.make_async_copy(own_ref, slot(panel, me), local)
        keep.start()
        pl.semaphore_wait(barrier, len(peers))
        order = sorted(range(groups), key=lambda g: abs(g - me))

        def spread_out(d):
            g = order[d]
            if d:
                arrive(panel, g)
            for side, target in enumerate((me - 1, me + 1)):
                onward = g >= me if side == 0 else g <= me
                if onward and 0 <= target < groups:
                    send(panel, g, send_z.at[side, g], (target, panel))
            send(panel, g, send_x.at[d], (me, east))
            send(panel, g, send_y.at[d], (me, north))
            send(panel, g, send_core.at[0, d], (me, mate))

        def pass_on(d):
            g = order[d]
            arrive(forward_from, g)
            send(forward_from, g, send_on.at[d], (me, forward_to))
            send(forward_from, g, send_core.at[1, d], (me, mate))
            arrive(forward_to, g)
            send(forward_to, g, send_core.at[2, d], (me, mate))

        spread_out(0)
        for d in range(groups):
            if d + 1 < groups:
                spread_out(d + 1)
            pass_on(d)
        for d, g in enumerate(order):
            arrive(across, g)
            send(across, g, send_core.at[3, d], (me, mate))
        for p in (mate,) + relatives(mate)[1:] + (relatives(across)[0],):
            for g in order:
                arrive(p, g)
        for item in sent:
            item.wait_send()
        keep.wait()

    for me in range(groups):
        pl.when(group == me)(functools.partial(run, me))


def gather(own, groups, panels):
    part = own.shape[1]
    any_space = pl.BlockSpec(memory_space=pl.ANY)
    dma = pltpu.SemaphoreType.DMA
    return pl.pallas_call(
        gather_kernel,
        out_shape=jax.ShapeDtypeStruct(
            (panels, own.shape[0], groups * part) + own.shape[2:], own.dtype
        ),
        in_specs=[any_space],
        out_specs=any_space,
        scratch_shapes=[
            dma((2, groups)), dma((groups,)), dma((groups,)), dma((groups,)),
            dma((4, groups)), dma((panels, groups)), dma,
        ],
        compiler_params=pltpu.CompilerParams(collective_id=0, has_side_effects=True),
    )(own)


def exchange_kernel(part_ref, out_ref, send, recv, local):
    group, panel = lax.axis_index("group"), lax.axis_index("panel")
    groups = lax.axis_size("group")
    part = out_ref.shape[2]
    barrier = pltpu.get_barrier_semaphore()
    peers = [lax.rem(group + d, groups) for d in range(1, groups)]
    for peer in peers:
        pl.semaphore_signal(barrier, inc=1, device_id=(peer, panel), device_id_type=MESH)
    keep = pltpu.make_async_copy(part_ref.at[:, pl.ds(group * part, part)], out_ref.at[0], local)
    keep.start()
    pl.semaphore_wait(barrier, len(peers))
    copies = [
        pltpu.make_async_remote_copy(
            src_ref=part_ref.at[:, pl.ds(peer * part, part)],
            dst_ref=out_ref.at[d + 1],
            send_sem=send.at[d],
            recv_sem=recv.at[d],
            device_id=(peer, panel),
            device_id_type=MESH,
        )
        for d, peer in enumerate(peers)
    ]
    for copy in copies:
        copy.start()
    for copy in copies:
        copy.wait()
    keep.wait()


def exchange(parts, groups):
    any_space = pl.BlockSpec(memory_space=pl.ANY)
    dma = pltpu.SemaphoreType.DMA
    slots, rows = parts.shape[0], parts.shape[1]
    return pl.pallas_call(
        exchange_kernel,
        out_shape=jax.ShapeDtypeStruct(
            (groups, slots, rows // groups) + parts.shape[2:], parts.dtype
        ),
        in_specs=[any_space],
        out_specs=any_space,
        scratch_shapes=[dma((groups - 1,)), dma((groups - 1,)), dma],
        compiler_params=pltpu.CompilerParams(collective_id=1, has_side_effects=True),
    )(parts)


def product_kernel(
    nodes_ref, trig_ref, weight_ref, whole_ref, spread_ref, share_ref, out_ref,
    a_ref, buf, acc, total_ref, sems, a_sems, out_sem,
):
    blocks, pieces, rows, kb = a_ref.shape
    depth, cols = buf.shape[0], buf.shape[2]
    b_ref = share_ref.reshape(share_ref.shape[0], 2 * blocks * kb, cols)
    first = lax.axis_index("group") * share_ref.shape[0]
    below, count = jnp.int32(0), jnp.int32(0)
    for t in range(nodes_ref.shape[0]):
        node = nodes_ref[t]
        below += (node < first).astype(jnp.int32)
        count += ((node >= first) & (node < first + share_ref.shape[0])).astype(jnp.int32)
    total = count * blocks

    def listed(step):
        return nodes_ref[below + step // blocks]

    def copy(step):
        start = pl.multiple_of((step % blocks) * 2 * kb, 2 * kb)
        slot = step % depth
        return pltpu.make_async_copy(
            b_ref.at[listed(step) - first, pl.ds(start, 2 * kb)], buf.at[slot], sems.at[slot]
        )

    def take(block):
        return pltpu.make_async_copy(
            whole_ref.at[block].reshape(pieces, rows, kb), a_ref.at[block], a_sems.at[block]
        )

    def fetch(step):
        @pl.when(step < total)
        def _():
            copy(step).start()

    fetch(0)
    for block in range(blocks):
        take(block).start()
    for step in range(1, depth - 1):
        fetch(step)
    total_ref[...] = jnp.zeros_like(total_ref)
    for block in range(blocks):
        take(block).wait()

    def body(step, carry):
        fetch(step + depth - 1)
        copy(step).wait()
        node = listed(step)
        point = node - first
        block = step % blocks
        slot = step % depth
        real = jnp.zeros((rows, kb), jnp.float32)
        imag = jnp.zeros((rows, kb), jnp.float32)
        for e in range(pieces):
            piece = a_ref[block, e].astype(jnp.float32)
            real = real + piece * trig_ref[node, e]
            imag = imag + piece * trig_ref[node, pieces + e]
        real = real.astype(jnp.bfloat16)
        imag = imag.astype(jnp.bfloat16)
        parts = []
        for t in range(kb // LANES):
            r = real[:, t * LANES : (t + 1) * LANES]
            i = imag[:, t * LANES : (t + 1) * LANES]
            parts.append(jnp.concatenate([r, -i], axis=1))
            parts.append(jnp.concatenate([i, r], axis=1))
        mixed = jnp.dot(
            jnp.concatenate(parts, axis=0), spread_ref[...], preferred_element_type=jnp.float32
        ).astype(jnp.bfloat16)
        left = jnp.concatenate(
            [mixed[2 * rows * t : 2 * rows * (t + 1)] for t in range(kb // LANES)], axis=1
        )
        product = jnp.dot(left, buf[slot], preferred_element_type=jnp.float32)
        acc[...] = jnp.where(block == 0, product, acc[...] + product)

        @pl.when(block == blocks - 1)
        def _():
            for e in range(4):
                total_ref[e] += (
                    weight_ref[point, e] * acc[:rows] - weight_ref[point, 4 + e] * acc[rows:]
                )

        return carry

    lax.fori_loop(0, total, body, 0)
    done = pltpu.make_async_copy(total_ref, out_ref.reshape(*total_ref.shape), out_sem)
    done.start()
    done.wait()


def weighted_product(nodes, weight, whole, shares):
    cols = shares.shape[3]
    blocks, pieces, row_tiles, tile, kb = whole.shape
    rows = row_tiles * tile
    index = np.arange(2 * LANES)
    target = np.where(index < LANES, 2 * index, 2 * (index - LANES) + 1)
    spread = target[:, None] == index[None, :]
    power = (np.arange(4)[None, :] + 8 * np.arange(2)[:, None]).reshape(1, 8)
    turn = np.arange(NODE_NUMBER)[:, None] * power % NODE_NUMBER
    phase = TWO_PI_RADIANS * turn / NODE_NUMBER
    trig = np.concatenate([np.cos(phase), np.sin(phase)], axis=1)
    smem = pl.BlockSpec(memory_space=pltpu.SMEM)
    any_space = pl.BlockSpec(memory_space=pl.ANY)
    return pl.pallas_call(
        product_kernel,
        out_shape=jax.ShapeDtypeStruct((4, row_tiles, tile, cols), jnp.float32),
        in_specs=[
            smem, smem, smem, any_space, pl.BlockSpec(memory_space=pltpu.VMEM), any_space,
        ],
        out_specs=any_space,
        scratch_shapes=[
            pltpu.VMEM((blocks, pieces, rows, kb), jnp.bfloat16),
            pltpu.VMEM((DEPTH, 2 * kb, cols), jnp.bfloat16),
            pltpu.VMEM((2 * rows, cols), jnp.float32),
            pltpu.VMEM((4, rows, cols), jnp.float32),
            pltpu.SemaphoreType.DMA((DEPTH,)),
            pltpu.SemaphoreType.DMA((blocks,)),
            pltpu.SemaphoreType.DMA,
        ],
        compiler_params=pltpu.CompilerParams(vmem_limit_bytes=63 << 20),
    )(nodes, jnp.asarray(trig, jnp.float32), weight, whole, jnp.asarray(spread, jnp.bfloat16), shares)


def shards(own_kernels, groups, panels, source_matrix_tiles, shares, responding_nodes):
    here, cols = shares.shape[0], shares.shape[3]
    weight = local_weights(responding_nodes, here)
    _, rows, _, kb = source_matrix_tiles.shape
    tile = math.gcd(rows, 4)
    own = source_matrix_tiles.transpose(0, 2, 1, 3).reshape(8, rows // tile, tile, kb)
    if own_kernels:
        whole = gather(own, groups, panels)
    else:
        whole = lax.all_gather(own, "group", axis=1, tiled=True)
        whole = lax.all_gather(whole, "panel", axis=0)
    parts = weighted_product(responding_nodes, weight, whole, shares)
    if own_kernels:
        result = jnp.sum(exchange(parts, groups), axis=0)
    else:
        result = lax.psum_scatter(parts, "group", scatter_dimension=1, tiled=True)
    return result.reshape(2, 2, rows, cols).transpose(0, 2, 1, 3)


def solution(mesh):
    placed = (P(None, "group", None, "panel"), P("group", None, None, "panel"), P())
    groups, panels = mesh.shape["group"], mesh.shape["panel"]
    return jax.shard_map(
        functools.partial(shards, panels == 8, groups, panels),
        mesh=mesh,
        in_specs=placed,
        out_specs=P(None, "group", None, "panel"),
        check_vma=False,
    )
```
